32 devices in a mesh: ctx: 16 (over z, y, core), grp: 2 (over x).
Axes of the slice: x: 2, y: 2, z: 4, core: 2. Of those that a mesh axis runs over, the one named last changes fastest.
Arguments:
- query_in: bfloat16 [2560, 768], P(('grp', 'ctx')), parts along dimension 0, may hold values from -30 to 30
- key_in: bfloat16 [2560, 768], P(('grp', 'ctx')), parts along dimension 0, may hold values from -6 to 6
- value_in: bfloat16 [2560, 768], P(('grp', 'ctx')), parts along dimension 0, may hold values from -6 to 6
- length: int32 [2], P('grp'), parts along dimension 0, may hold values from 320 to 1280
- out_weight: bfloat16 [768, 1536], replicated, may hold values from -0.21875 to 0.21875
Outputs:
- projected: bfloat16 [2560, 1536], P(('grp', 'ctx')), parts along dimension 0
The draws below stay inside these ranges and needn't reach their ends.
There are 2 independent parts, one for each index of `grp`. The reference program is written for one: setup_inputs(seed, part) draws one part's arguments, and reference() takes and returns one part's arrays. A program takes and returns all parts, laid end to end along the dimension named above; an argument that names none is the same for every part. Nothing has to cross between parts.
All inputs are finite; a program needn't handle non-finite values.
Results may differ from the reference program's by a relative error of at most 0.007.
Values may be sent and summed in bfloat16 or wider, within the bound.
A program may use at most 64 MiB of HBM per device.

```python
import jax
import jax.numpy as jnp
from jax import lax

HEADS = 12
HDIM = 64
D = 1536
CIN = 768
FRAMES = 1280


def draw_pair(base):
    seeded = jax.random.fold_in(base, 11)
    first_key, second_key = jax.random.split(seeded, 2)
    full_shape = (FRAMES, HEADS * HDIM)
    queries = jnp.clip(jax.random.normal(first_key, full_shape, jnp.float32), -6.0, 6.0)
    keyset = jnp.clip(jax.random.normal(second_key, full_shape, jnp.float32), -6.0, 6.0)
    return (queries, keyset)


def draw_query_in(key, part):
    return draw_pair(key)[0].astype(jnp.bfloat16)


def draw_key_in(key, part):
    return draw_pair(key)[1].astype(jnp.bfloat16)


def steps_of(own_key, dims, cuts, low, top_value):
    loudness = 1.0
    for axis_at, parts in cuts:
        heights = jax.random.uniform(jax.random.fold_in(jax.random.fold_in(own_key, 6), axis_at), (parts,), jnp.float32, low / len(cuts), top_value / len(cuts))
        loudness = loudness * jnp.repeat(jnp.exp(heights), dims[axis_at] // parts).reshape((-1,) + (1,) * (len(dims) - 1 - axis_at))
    return loudness


def normal_values(stream_key, dims, width, bound, pieces=(), kind=jnp.bfloat16):
    loudness = steps_of(stream_key, dims, pieces, -0.22, 0.18) if pieces else 1.0
    entries = jax.random.normal(stream_key, dims, jnp.float32) * width * loudness
    return jnp.minimum(jnp.maximum(entries, -bound), bound).astype(kind)


def setup_inputs(seed: int = 0, part: int = 0) -> dict:
    splits = jax.random.split(jax.random.key(seed), 6)
    own_keys = jax.random.split(jax.random.fold_in(splits[5], part), 6)
    query_in = draw_query_in(jax.random.fold_in(jax.random.fold_in(splits[5], part), 71), part)
    key_in = draw_key_in(jax.random.fold_in(jax.random.fold_in(splits[5], part), 71), part)
    value_in = normal_values(own_keys[2], (FRAMES, CIN), 1.0, 6.0, ((0, 16),))
    length = jax.random.randint(own_keys[3], (1,), FRAMES // 4, FRAMES + 1).astype(jnp.int32)
    out_weight = normal_values(splits[4], (CIN, D), CIN ** -0.5, 0.21875)
    return {"query_in": query_in, "key_in": key_in, "value_in": value_in, "length": length, "out_weight": out_weight}


def reference(query_in, key_in, value_in, length, out_weight):
    frame_count = query_in.shape[0]
    valid_len = length[0]
    positions = jnp.arange(frame_count, dtype=jnp.int32)
    key_live = positions < valid_len
    score_scale = 1.0 / jnp.sqrt(jnp.float32(HDIM))
    query_heads = query_in.reshape(frame_count, HEADS, HDIM).transpose(1, 0, 2)
    key_heads = key_in.reshape(frame_count, HEADS, HDIM).transpose(1, 0, 2)
    value_heads = value_in.reshape(frame_count, HEADS, HDIM).transpose(1, 0, 2)

    def one_head(operands):
        query_h, key_h, value_h = operands
        scores = jnp.dot(query_h, key_h.T, preferred_element_type=jnp.float32) * score_scale
        running = lax.optimization_barrier(jnp.max(jnp.where(key_live[None, :], scores, jnp.float32(-1e+30)), axis=1))
        expons = jnp.where(key_live[None, :], jnp.exp(scores - running[:, None]), jnp.float32(0.0))
        denominator = lax.optimization_barrier(jnp.sum(expons, axis=1))
        weighted = jnp.dot(expons.astype(jnp.bfloat16), value_h, preferred_element_type=jnp.float32)
        return weighted / denominator[:, None]
    heads_out = lax.map(one_head, (query_heads, key_heads, value_heads))
    attended = heads_out.transpose(1, 0, 2).reshape(frame_count, HEADS * HDIM)
    attended = jnp.where(key_live[:, None], attended, jnp.float32(0.0)).astype(jnp.bfloat16)
    return jnp.dot(attended, out_weight, preferred_element_type=jnp.float32).astype(jnp.bfloat16)
```

```python
import functools

import jax
import jax.numpy as jnp
from jax import lax
from jax.experimental import pallas as pl
from jax.experimental.pallas import tpu as pltpu
from jax.sharding import PartitionSpec as P

HEADS = 12
HDIM = 64
LEVELS = 4
MESH = pl.DeviceIdType.MESH
NT = (((1,), (1,)), ((), ()))


def kernel(
    n, q_ref, k_ref, v_ref, len_ref, w_hbm, out_ref,
    send_q, send_k, send_v, q_buf, k_buf, v_buf, o_send, o_buf, w_buf,
    w_sem, sq_sem, rq_sem, sk_sem, rk_sem, sv_sem, rv_sem, so_sem, ro_sem,
):
    rows = q_ref.shape[0]
    cols = n // LEVELS
    chips = cols // 2
    me = lax.axis_index("ctx")
    level, col = me // cols, me % cols
    core = col % 2
    sibling = level * cols + col + 1 - 2 * core

    def mate(off):
        return ((level + off) % LEVELS) * cols + col

    def chip_col(off):
        return (col + 2 * off) % cols

    w_copy = pltpu.make_async_copy(w_hbm, w_buf, w_sem)
    w_copy.start()

    barrier = pltpu.get_barrier_semaphore()
    greeted = [mate(off) for off in range(1, LEVELS)] + [sibling]
    greeted += [level * cols + chip_col(off) for off in range(1, chips)]
    for other in greeted:
        pl.semaphore_signal(barrier, inc=1, device_id={"ctx": other}, device_id_type=MESH)

    scale = jnp.asarray(HDIM ** -0.5, jnp.bfloat16)
    for d in range(LEVELS):
        pair = slice(128 * d, 128 * d + 128)
        one = slice(512 + 64 * d, 576 + 64 * d)
        send_k[d, :, :128] = k_ref[:, pair]
        send_k[d, :, 128:] = jnp.concatenate([k_ref[:, one], v_ref[:, one]], axis=1)
        send_q[d, :, :128] = q_ref[:, pair] * scale
        q_one = q_ref[:, one] * scale
        send_q[d, :, 128:] = jnp.concatenate([q_one, jnp.zeros_like(q_one)], axis=1)
        send_v[d] = v_ref[:, pair]
    k_buf[me] = send_k[level]
    v_buf[me] = send_v[level]
    q_buf[level] = send_q[level]

    pl.semaphore_wait(barrier, len(greeted))

    sent = []

    def remote(src, dst, send_sem, recv_sem, target):
        copy = pltpu.make_async_remote_copy(
            src_ref=src, dst_ref=dst, send_sem=send_sem, recv_sem=recv_sem,
            device_id={"ctx": target}, device_id_type=MESH,
        )
        copy.start()
        sent.append(copy)

    def arrived(buf, slot, sem):
        pltpu.make_async_remote_copy(
            src_ref=buf.at[slot], dst_ref=buf.at[slot], send_sem=sem.at[slot], recv_sem=sem.at[slot],
            device_id={"ctx": sibling}, device_id_type=MESH,
        ).wait_recv()

    used = {"k": 0, "v": 0}

    def forward(kind, slot, target):
        buf, send, recv = (k_buf, sk_sem, rk_sem) if kind == "k" else (v_buf, sv_sem, rv_sem)
        remote(buf.at[slot], buf.at[slot], send.at[used[kind]], recv.at[slot], target)
        used[kind] += 1

    def phase_one(kind, off):
        buf, src, send, recv = (
            (k_buf, send_k, sk_sem, rk_sem) if kind == "k" else (v_buf, send_v, sv_sem, rv_sem)
        )
        other = (level + off) % LEVELS
        remote(src.at[other], buf.at[me], send.at[used[kind]], recv.at[me], mate(off))
        used[kind] += 1

    def spread(kind, slot):
        for off in range(1, chips):
            forward(kind, slot, level * cols + chip_col(off))
        forward(kind, slot, sibling)

    order = (2, 1, 3)
    for off in order:
        other = (level + off) % LEVELS
        phase_one("k", off)
        remote(send_q.at[other], q_buf.at[level], sq_sem.at[off], rq_sem.at[level], mate(off))
    spread("k", me)
    for off in order:
        phase_one("v", off)
    spread("v", me)

    def source(off):
        return (level - off + LEVELS) % LEVELS

    buffers = {"k": (k_buf, rk_sem), "v": (v_buf, rv_sem)}
    for kind in ("k", "v"):
        buf, sem = buffers[kind]
        for off in (0,) + order:
            if off:
                slot = source(off) * cols + col
                arrived(buf, slot, sem)
                spread(kind, slot)
        for off in (0,) + order:
            for hop in range(1, chips):
                slot = source(off) * cols + chip_col(hop)
                arrived(buf, slot, sem)
                forward(kind, slot, sibling)
    for kind in ("k", "v"):
        buf, sem = buffers[kind]
        for off in (0,) + order:
            for hop in range(chips):
                arrived(buf, source(off) * cols + chip_col(hop) + 1 - 2 * core, sem)
    for off in order:
        arrived(q_buf, source(off), rq_sem)

    valid = len_ref[0]
    frames = n * rows
    live = lax.broadcasted_iota(jnp.int32, (1, frames), 1) < valid
    low = lax.broadcasted_iota(jnp.int32, (1, 128), 1) < HDIM
    k_pair = k_buf[:, :, :128].reshape(frames, 128)
    kv_one = k_buf[:, :, 128:].reshape(frames, 128)
    v_pair = v_buf[...].reshape(frames, 128)

    def attend(q, k, v):
        s = lax.dot_general(q, k, NT, preferred_element_type=jnp.float32)
        s = jnp.where(live, s, jnp.float32(-1e30))
        e = jnp.exp(s - jnp.max(s, axis=1, keepdims=True))
        total = jnp.sum(e, axis=1, keepdims=True)
        return jnp.dot(e.astype(jnp.bfloat16), v, preferred_element_type=jnp.float32) / total

    for off in order + (0,):
        j = (level + off) % LEVELS
        q_pair = q_buf[j, :, :128]
        zero = jnp.zeros_like(q_pair)
        q_two = jnp.concatenate([jnp.where(low, q_pair, zero), jnp.where(low, zero, q_pair)], axis=0)
        o_two = attend(q_two, k_pair, v_pair)
        o_one = attend(q_buf[j, :, 128:], kv_one, kv_one)
        row = (j * cols + col) * rows + lax.broadcasted_iota(jnp.int32, (rows, 1), 0)
        keep = row < valid
        none = jnp.float32(0.0)
        o_pair = jnp.where(keep, jnp.where(low, o_two[:rows], o_two[rows:]), none).astype(jnp.bfloat16)
        o_one = jnp.where(keep, o_one, none).astype(jnp.bfloat16)
        if off:
            o_send[off - 1, :, :128] = o_pair
            o_send[off - 1, :, 128:] = o_one
            remote(o_send.at[off - 1], o_buf.at[level], so_sem.at[off - 1], ro_sem.at[level], mate(off))
        else:
            o_buf[level, :, :128] = o_pair
            o_buf[level, :, 128:] = o_one

    for off in order:
        arrived(o_buf, source(off), ro_sem)
    parts = [o_buf[g, :, :128] for g in range(LEVELS)]
    for g in range(0, LEVELS, 2):
        parts.append(
            jnp.concatenate([o_buf[g, :, 192:], o_buf[g + 1, :, 192:]], axis=1)
        )
    w_copy.wait()
    attended = jnp.concatenate(parts, axis=1)
    out_ref[...] = jnp.dot(attended, w_buf[...], preferred_element_type=jnp.float32).astype(jnp.bfloat16)
    for copy in sent:
        copy.wait_send()


def body(n, query_in, key_in, value_in, length, out_weight):
    rows, cin = query_in.shape
    width = out_weight.shape[1]
    bf = jnp.bfloat16
    chips = n // LEVELS // 2
    copies = (LEVELS - 1) + LEVELS * chips + LEVELS * (chips - 1)
    dma = pltpu.SemaphoreType.DMA
    vmem = pl.BlockSpec(memory_space=pltpu.VMEM)
    return pl.pallas_call(
        functools.partial(kernel, n),
        out_shape=jax.ShapeDtypeStruct((rows, width), bf),
        in_specs=[vmem, vmem, vmem, pl.BlockSpec(memory_space=pltpu.SMEM), pl.BlockSpec(memory_space=pl.ANY)],
        out_specs=vmem,
        scratch_shapes=[
            pltpu.VMEM((LEVELS, rows, 256), bf),
            pltpu.VMEM((LEVELS, rows, 256), bf),
            pltpu.VMEM((LEVELS, rows, 128), bf),
            pltpu.VMEM((LEVELS, rows, 256), bf),
            pltpu.VMEM((n, rows, 256), bf),
            pltpu.VMEM((n, rows, 128), bf),
            pltpu.VMEM((LEVELS - 1, rows, 256), bf),
            pltpu.VMEM((LEVELS, rows, 256), bf),
            pltpu.VMEM((cin, width), bf),
            dma,
            dma((LEVELS,)),
            dma((LEVELS,)),
            dma((copies,)),
            dma((n,)),
            dma((copies,)),
            dma((n,)),
            dma((LEVELS,)),
            dma((LEVELS,)),
        ],
        compiler_params=pltpu.CompilerParams(
            collective_id=0, has_side_effects=True, vmem_limit_bytes=48 * 2**20
        ),
        name="attention",
    )(query_in, key_in, value_in, length, out_weight)


def solution(mesh):
    split = P(("grp", "ctx"), None)
    return jax.shard_map(
        functools.partial(body, mesh.shape["ctx"]),
        mesh=mesh,
        in_specs=(split, split, split, P("grp"), P()),
        out_specs=split,
        check_vma=False,
    )
```

```python
import functools

import jax
import jax.numpy as jnp
from jax import lax
from jax.experimental import pallas as pl
from jax.experimental.pallas import tpu as pltpu
from jax.sharding import PartitionSpec as P

HEADS = 12
HDIM = 64
LEVELS = 4
MESH = pl.DeviceIdType.MESH
NT = (((1,), (1,)), ((), ()))


def kernel(
    n, q_hbm, k_hbm, v_hbm, len_ref, w_hbm, out_ref,
    q_ref, k_ref, v_ref, send_q, send_k, send_v, q_buf, k_buf, v_buf, o_send, o_buf, w_buf,
    in_sem, w_sem, sq_sem, rq_sem, sk_sem, rk_sem, sv_sem, rv_sem, so_sem, ro_sem,
):
    rows = q_ref.shape[0]
    cols = n // LEVELS
    chips = cols // 2
    me = lax.axis_index("ctx")
    level, col = me // cols, me % cols
    core = col % 2
    sibling = level * cols + col + 1 - 2 * core

    def mate(off):
        return ((level + off) % LEVELS) * cols + col

    def chip_col(off):
        return (col + 2 * off) % cols

    loads = [
        pltpu.make_async_copy(src, dst, in_sem.at[i])
        for i, (src, dst) in enumerate(((k_hbm, k_ref), (q_hbm, q_ref), (v_hbm, v_ref)))
    ]
    for load in loads:
        load.start()
    w_copy = pltpu.make_async_copy(w_hbm, w_buf, w_sem)
    w_copy.start()

    barrier = pltpu.get_barrier_semaphore()
    greeted = [mate(off) for off in range(1, LEVELS)] + [sibling]
    greeted += [level * cols + chip_col(off) for off in range(1, chips)]
    for other in greeted:
        pl.semaphore_signal(barrier, inc=1, device_id={"ctx": other}, device_id_type=MESH)

    for load in loads:
        load.wait()

    scale = jnp.asarray(HDIM ** -0.5, jnp.bfloat16)
    for d in range(LEVELS):
        pair = slice(128 * d, 128 * d + 128)
        one = slice(512 + 64 * d, 576 + 64 * d)
        send_k[d, :, :128] = k_ref[:, pair]
        send_k[d, :, 128:] = jnp.concatenate([k_ref[:, one], v_ref[:, one]], axis=1)
        send_q[d, :, :128] = q_ref[:, pair] * scale
        q_one = q_ref[:, one] * scale
        send_q[d, :, 128:] = jnp.concatenate([q_one, jnp.zeros_like(q_one)], axis=1)
        send_v[d] = v_ref[:, pair]
    k_buf[me] = send_k[level]
    v_buf[me] = send_v[level]
    q_buf[level] = send_q[level]

    pl.semaphore_wait(barrier, len(greeted))

    sent = []

    def remote(src, dst, send_sem, recv_sem, target):
        copy = pltpu.make_async_remote_copy(
            src_ref=src, dst_ref=dst, send_sem=send_sem, recv_sem=recv_sem,
            device_id={"ctx": target}, device_id_type=MESH,
        )
        copy.start()
        sent.append(copy)

    def arrived(buf, slot, sem):
        pltpu.make_async_remote_copy(
            src_ref=buf.at[slot], dst_ref=buf.at[slot], send_sem=sem.at[slot], recv_sem=sem.at[slot],
            device_id={"ctx": sibling}, device_id_type=MESH,
        ).wait_recv()

    used = {"k": 0, "v": 0}

    def forward(kind, slot, target):
        buf, send, recv = (k_buf, sk_sem, rk_sem) if kind == "k" else (v_buf, sv_sem, rv_sem)
        remote(buf.at[slot], buf.at[slot], send.at[used[kind]], recv.at[slot], target)
        used[kind] += 1

    def phase_one(kind, off):
        buf, src, send, recv = (
            (k_buf, send_k, sk_sem, rk_sem) if kind == "k" else (v_buf, send_v, sv_sem, rv_sem)
        )
        other = (level + off) % LEVELS
        remote(src.at[other], buf.at[me], send.at[used[kind]], recv.at[me], mate(off))
        used[kind] += 1

    def spread(kind, slot):
        for off in range(1, chips):
            forward(kind, slot, level * cols + chip_col(off))
        forward(kind, slot, sibling)

    order = (2, 1, 3)
    for off in order:
        other = (level + off) % LEVELS
        phase_one("k", off)
        remote(send_q.at[other], q_buf.at[level], sq_sem.at[off], rq_sem.at[level], mate(off))
    spread("k", me)
    for off in order:
        phase_one("v", off)
    spread("v", me)

    def source(off):
        return (level - off + LEVELS) % LEVELS

    buffers = {"k": (k_buf, rk_sem), "v": (v_buf, rv_sem)}
    for kind in ("k", "v"):
        buf, sem = buffers[kind]
        for off in (0,) + order:
            if off:
                slot = source(off) * cols + col
                arrived(buf, slot, sem)
                spread(kind, slot)
        for off in (0,) + order:
            for hop in range(1, chips):
                slot = source(off) * cols + chip_col(hop)
                arrived(buf, slot, sem)
                forward(kind, slot, sibling)
    for kind in ("k", "v"):
        buf, sem = buffers[kind]
        for off in (0,) + order:
            for hop in range(chips):
                arrived(buf, source(off) * cols + chip_col(hop) + 1 - 2 * core, sem)
    for off in order:
        arrived(q_buf, source(off), rq_sem)

    valid = len_ref[0]
    frames = n * rows
    live = lax.broadcasted_iota(jnp.int32, (1, frames), 1) < valid
    low = lax.broadcasted_iota(jnp.int32, (1, 128), 1) < HDIM
    k_pair = k_buf[:, :, :128].reshape(frames, 128)
    kv_one = k_buf[:, :, 128:].reshape(frames, 128)
    v_pair = v_buf[...].reshape(frames, 128)

    def attend(q, k, v):
        s = lax.dot_general(q, k, NT, preferred_element_type=jnp.float32)
        s = jnp.where(live, s, jnp.float32(-1e30))
        e = jnp.exp(s - jnp.max(s, axis=1, keepdims=True))
        total = jnp.sum(e, axis=1, keepdims=True)
        return jnp.dot(e.astype(jnp.bfloat16), v, preferred_element_type=jnp.float32) / total

    for off in order + (0,):
        j = (level + off) % LEVELS
        q_pair = q_buf[j, :, :128]
        zero = jnp.zeros_like(q_pair)
        q_two = jnp.concatenate([jnp.where(low, q_pair, zero), jnp.where(low, zero, q_pair)], axis=0)
        o_two = attend(q_two, k_pair, v_pair)
        o_one = attend(q_buf[j, :, 128:], kv_one, kv_one)
        row = (j * cols + col) * rows + lax.broadcasted_iota(jnp.int32, (rows, 1), 0)
        keep = row < valid
        none = jnp.float32(0.0)
        o_pair = jnp.where(keep, jnp.where(low, o_two[:rows], o_two[rows:]), none).astype(jnp.bfloat16)
        o_one = jnp.where(keep, o_one, none).astype(jnp.bfloat16)
        if off:
            o_send[off - 1, :, :128] = o_pair
            o_send[off - 1, :, 128:] = o_one
            remote(o_send.at[off - 1], o_buf.at[level], so_sem.at[off - 1], ro_sem.at[level], mate(off))
        else:
            o_buf[level, :, :128] = o_pair
            o_buf[level, :, 128:] = o_one

    for off in order:
        arrived(o_buf, source(off), ro_sem)
    parts = [o_buf[g, :, :128] for g in range(LEVELS)]
    for g in range(0, LEVELS, 2):
        parts.append(
            jnp.concatenate([o_buf[g, :, 192:], o_buf[g + 1, :, 192:]], axis=1)
        )
    w_copy.wait()
    attended = jnp.concatenate(parts, axis=1)
    out_ref[...] = jnp.dot(attended, w_buf[...], preferred_element_type=jnp.float32).astype(jnp.bfloat16)
    for copy in sent:
        copy.wait_send()


def body(n, query_in, key_in, value_in, length, out_weight):
    rows, cin = query_in.shape
    width = out_weight.shape[1]
    bf = jnp.bfloat16
    chips = n // LEVELS // 2
    copies = (LEVELS - 1) + LEVELS * chips + LEVELS * (chips - 1)
    dma = pltpu.SemaphoreType.DMA
    vmem = pl.BlockSpec(memory_space=pltpu.VMEM)
    hbm = pl.BlockSpec(memory_space=pl.ANY)
    return pl.pallas_call(
        functools.partial(kernel, n),
        out_shape=jax.ShapeDtypeStruct((rows, width), bf),
        in_specs=[hbm, hbm, hbm, pl.BlockSpec(memory_space=pltpu.SMEM), hbm],
        out_specs=vmem,
        scratch_shapes=[
            pltpu.VMEM((rows, cin), bf),
            pltpu.VMEM((rows, cin), bf),
            pltpu.VMEM((rows, cin), bf),
            pltpu.VMEM((LEVELS, rows, 256), bf),
            pltpu.VMEM((LEVELS, rows, 256), bf),
            pltpu.VMEM((LEVELS, rows, 128), bf),
            pltpu.VMEM((LEVELS, rows, 256), bf),
            pltpu.VMEM((n, rows, 256), bf),
            pltpu.VMEM((n, rows, 128), bf),
            pltpu.VMEM((LEVELS - 1, rows, 256), bf),
            pltpu.VMEM((LEVELS, rows, 256), bf),
            pltpu.VMEM((cin, width), bf),
            dma((3,)),
            dma,
            dma((LEVELS,)),
            dma((LEVELS,)),
            dma((copies,)),
            dma((n,)),
            dma((copies,)),
            dma((n,)),
            dma((LEVELS,)),
            dma((LEVELS,)),
        ],
        compiler_params=pltpu.CompilerParams(
            collective_id=0, has_side_effects=True, vmem_limit_bytes=63 * 2**20
        ),
        name="attention",
    )(query_in, key_in, value_in, length, out_weight)


def solution(mesh):
    split = P(("grp", "ctx"), None)
    return jax.shard_map(
        functools.partial(body, mesh.shape["ctx"]),
        mesh=mesh,
        in_specs=(split, split, split, P("grp"), P()),
        out_specs=split,
        check_vma=False,
    )
```

```python
import functools

import jax
import jax.numpy as jnp
from jax import lax
from jax.experimental import pallas as pl
from jax.experimental.pallas import tpu as pltpu
from jax.sharding import PartitionSpec as P

HEADS = 12
HDIM = 64
LEVELS = 4
PAIRS = 2 * LEVELS * HDIM
MESH = pl.DeviceIdType.MESH
NT = (((1,), (1,)), ((), ()))
F32 = jnp.float32
BF16 = jnp.bfloat16
FAR_FIRST = (2, 1, 3)


def kernel(
    n, q_hbm, k_hbm, v_hbm, len_hbm, w_hbm, out_ref,
    len_ref, q_in, k_in, v_in, kv2, kv1, q2, q1, kv1_send, q1_send, o2, o1, o2_send, o1_send, w_buf,
    in_sem, own_sem, w_sem,
    one_send, kv2_recv, hop2_recv, hop2_send, kv1_recv, hop1_send, q2_recv, q1_recv, o2_recv, o1_recv,
):
    rows = out_ref.shape[0]
    half = rows // 2
    cols = n // LEVELS
    chips = cols // 2
    me = lax.axis_index("ctx")
    level, col = me // cols, me % cols
    core = col % 2
    flip = 1 - 2 * core
    sibling = me + flip
    low = lax.broadcasted_iota(jnp.int32, (1, 2 * HDIM), 1) < HDIM

    def up(off):
        return (level + off) % LEVELS

    def source(off):
        return (level + LEVELS - off) % LEVELS

    def chip_col(off):
        return (col + 2 * off) % cols

    def pair(ref, g):
        return ref.at[:, pl.ds(pl.multiple_of(g * 2 * HDIM, 2 * HDIM), 2 * HDIM)]

    local = [
        pltpu.make_async_copy(hbm.at[:, pl.ds(PAIRS, LEVELS * HDIM)], ref, in_sem.at[i])
        for i, (hbm, ref) in enumerate(((k_hbm, k_in), (v_hbm, v_in), (q_hbm, q_in)))
    ]
    own = [
        pltpu.make_async_copy(pair(k_hbm, level), kv2.at[me, 0], own_sem.at[0]),
        pltpu.make_async_copy(pair(v_hbm, level), kv2.at[me, 1], own_sem.at[1]),
        pltpu.make_async_copy(pair(q_hbm, level), q2.at[level], own_sem.at[2]),
        pltpu.make_async_copy(len_hbm, len_ref, own_sem.at[3]),
    ]
    w_copy = pltpu.make_async_copy(w_hbm, w_buf, w_sem)
    for copy in local + own:
        copy.start()

    barrier = pltpu.get_barrier_semaphore()
    greeted = [up(off) * cols + col for off in range(1, LEVELS)] + [sibling]
    greeted += [level * cols + chip_col(off) for off in range(1, chips)]
    for other in greeted:
        pl.semaphore_signal(barrier, inc=1, device_id={"ctx": other}, device_id_type=MESH)

    for copy in local:
        copy.wait()
    for g in range(LEVELS):
        one = slice(HDIM * g, HDIM * g + HDIM)
        kv1_send[g] = jnp.concatenate([k_in[:, one], v_in[:, one]], axis=1)
        q_one = q_in[:, one].astype(F32)
        q1_send[g] = jnp.concatenate([q_one[:half], q_one[half:]], axis=1).astype(BF16)
    kv1[me] = kv1_send[level]
    q1[level] = q1_send[level]

    pl.semaphore_wait(barrier, len(greeted))

    sent = []

    def remote(src, dst, send_sem, recv_sem, target):
        copy = pltpu.make_async_remote_copy(
            src_ref=src, dst_ref=dst, send_sem=send_sem, recv_sem=recv_sem,
            device_id={"ctx": target}, device_id_type=MESH,
        )
        copy.start()
        sent.append(copy)

    def arrived(buf, sem):
        pltpu.make_async_remote_copy(
            src_ref=buf, dst_ref=buf, send_sem=sem, recv_sem=sem,
            device_id={"ctx": sibling}, device_id_type=MESH,
        ).wait_recv()

    def send(src, dst, kind, off, recv_sem):
        remote(src, dst, one_send.at[kind, off], recv_sem, up(off) * cols + col)

    def send_pair(off):
        send(pair(k_hbm, up(off)), kv2.at[me, 0], 0, off, kv2_recv.at[level, 0])
        send(pair(v_hbm, up(off)), kv2.at[me, 1], 1, off, kv2_recv.at[level, 1])
        send(pair(q_hbm, up(off)), q2.at[level], 2, off, q2_recv.at[level])

    def send_single(off):
        send(kv1_send.at[up(off)], kv1.at[me], 3, off, kv1_recv.at[me])
        send(q1_send.at[up(off)], q1.at[level], 4, off, q1_recv.at[level])

    used = [0, 0]
    stages = ((kv2, hop2_send, hop2_recv), (kv1, hop1_send, kv1_recv))

    def forward(stage, slot, target):
        buf, send_sem, recv_sem = stages[stage]
        remote(buf.at[slot], buf.at[slot], send_sem.at[used[stage]], recv_sem.at[slot], target)
        used[stage] += 1

    def spread(stage, slot):
        for off in range(1, chips):
            forward(stage, slot, level * cols + chip_col(off))
        forward(stage, slot, sibling)

    def from_column(stage, off):
        slot = source(off) * cols + col
        if stage == 0:
            arrived(kv2.at[slot, 0], kv2_recv.at[source(off), 0])
            arrived(kv2.at[slot, 1], kv2_recv.at[source(off), 1])
        else:
            arrived(kv1.at[slot], kv1_recv.at[slot])
        spread(stage, slot)

    def from_chips(stage):
        buf, _, recv_sem = stages[stage]
        for off in (0,) + FAR_FIRST:
            for hop in range(1, chips):
                slot = source(off) * cols + chip_col(hop)
                arrived(buf.at[slot], recv_sem.at[slot])
                forward(stage, slot, sibling)

    def from_sibling(stage):
        buf, _, recv_sem = stages[stage]
        for off in (0,) + FAR_FIRST:
            for hop in range(chips):
                slot = source(off) * cols + chip_col(hop) + flip
                arrived(buf.at[slot], recv_sem.at[slot])

    for off in FAR_FIRST:
        send_pair(off)
    for copy in own:
        copy.wait()
    w_copy.start()
    spread(0, me)
    spread(1, me)
    for off in FAR_FIRST:
        send_single(off)
    for off in FAR_FIRST:
        from_column(0, off)
    for off in FAR_FIRST:
        from_column(1, off)
    from_chips(0)
    from_sibling(0)

    valid = len_ref[0]
    frames = n * rows
    scale = jnp.asarray(HDIM ** -0.5, BF16)
    live = lax.broadcasted_iota(jnp.int32, (1, frames), 1) < valid

    def attend(q, k, v):
        s = lax.dot_general(q, k, NT, preferred_element_type=F32)
        s = jnp.where(live, s, F32(-1e30))
        e = jnp.exp(s - jnp.max(s, axis=1, keepdims=True))
        total = jnp.sum(e, axis=1, keepdims=True)
        return jnp.dot(e.astype(BF16), v, preferred_element_type=F32) / total

    def keep(j, out):
        row = (j * cols + col) * rows + lax.broadcasted_iota(jnp.int32, (rows, 1), 0)
        return jnp.where(row < valid, out, F32(0.0))

    def attend_pair(off):
        j = up(off)
        if off:
            arrived(q2.at[j], q2_recv.at[j])
        q = q2[j] * scale
        zero = jnp.zeros_like(q)
        q = jnp.concatenate([jnp.where(low, q, zero), jnp.where(low, zero, q)], axis=0)
        out = attend(q, kv2[:, 0].reshape(frames, 2 * HDIM), kv2[:, 1].reshape(frames, 2 * HDIM))
        out = keep(j, jnp.where(low, out[:rows], out[rows:])).astype(BF16)
        if off:
            o2_send[off] = out
            send(o2_send.at[off], o2.at[level], 5, off, o2_recv.at[level])
        else:
            o2[level] = out

    def attend_single(off):
        j = up(off)
        if off:
            arrived(q1.at[j], q1_recv.at[j])
        q = q1[j].astype(F32)
        zero = jnp.zeros_like(q)
        q = jnp.concatenate(
            [jnp.where(low, q, zero), jnp.where(low, pltpu.roll(q, HDIM, 1), zero)], axis=0
        ).astype(BF16) * scale
        kv = kv1[...].reshape(frames, 2 * HDIM)
        out = keep(j, attend(q, kv, kv))
        out = jnp.where(low, pltpu.roll(out[half:], HDIM, 1), out[:half]).astype(BF16)
        if off:
            o1_send[off] = out
            send(o1_send.at[off], o1.at[level], 6, off, o1_recv.at[level])
        else:
            o1[level] = out

    attend_pair(FAR_FIRST[0])
    attend_pair(FAR_FIRST[1])
    from_chips(1)
    attend_pair(FAR_FIRST[2])
    attend_pair(0)
    from_sibling(1)
    for off in FAR_FIRST + (0,):
        attend_single(off)

    w_copy.wait()
    for off in FAR_FIRST:
        arrived(o2.at[source(off)], o2_recv.at[source(off)])
    pairs = jnp.concatenate([o2[g] for g in range(LEVELS)], axis=1)
    total = jnp.dot(pairs, w_buf[:PAIRS, :], preferred_element_type=F32)
    for off in FAR_FIRST:
        arrived(o1.at[source(off)], o1_recv.at[source(off)])
    parts = []
    for g in range(0, LEVELS, 2):
        even, odd = o1[g].astype(F32), o1[g + 1].astype(F32)
        top = jnp.where(low, pltpu.roll(even, HDIM, 1), odd)
        bottom = jnp.where(low, even, pltpu.roll(odd, HDIM, 1))
        parts.append(jnp.concatenate([top, bottom], axis=0).astype(BF16))
    singles = jnp.concatenate(parts, axis=1)
    total = total + jnp.dot(singles, w_buf[PAIRS:, :], preferred_element_type=F32)
    out_ref[...] = total.astype(BF16)
    for copy in sent:
        copy.wait_send()


def body(n, query_in, key_in, value_in, length, out_weight):
    rows, cin = query_in.shape
    width = out_weight.shape[1]
    chips = n // LEVELS // 2
    hops = LEVELS * chips + LEVELS * (chips - 1)
    lanes = 2 * HDIM
    dma = pltpu.SemaphoreType.DMA
    hbm = pl.BlockSpec(memory_space=pl.ANY)

    def vmem(*shape):
        return pltpu.VMEM(shape, BF16)

    return pl.pallas_call(
        functools.partial(kernel, n),
        out_shape=jax.ShapeDtypeStruct((rows, width), BF16),
        in_specs=[hbm] * 5,
        out_specs=pl.BlockSpec(memory_space=pltpu.VMEM),
        scratch_shapes=[
            pltpu.SMEM((1,), jnp.int32),
            vmem(rows, LEVELS * HDIM),
            vmem(rows, LEVELS * HDIM),
            vmem(rows, LEVELS * HDIM),
            vmem(n, 2, rows, lanes),
            vmem(n, rows, lanes),
            vmem(LEVELS, rows, lanes),
            vmem(LEVELS, rows // 2, lanes),
            vmem(LEVELS, rows, lanes),
            vmem(LEVELS, rows // 2, lanes),
            vmem(LEVELS, rows, lanes),
            vmem(LEVELS, rows // 2, lanes),
            vmem(LEVELS, rows, lanes),
            vmem(LEVELS, rows // 2, lanes),
            vmem(cin, width),
            dma((3,)),
            dma((4,)),
            dma,
            dma((7, LEVELS)),
            dma((LEVELS, 2)),
            dma((n,)),
            dma((hops,)),
            dma((n,)),
            dma((hops,)),
            dma((LEVELS,)),
            dma((LEVELS,)),
            dma((LEVELS,)),
            dma((LEVELS,)),
        ],
        compiler_params=pltpu.CompilerParams(
            collective_id=0, has_side_effects=True, vmem_limit_bytes=63 * 2**20
        ),
        name="attention",
    )(query_in, key_in, value_in, length, out_weight)


def solution(mesh):
    split = P(("grp", "ctx"), None)
    return jax.shard_map(
        functools.partial(body, mesh.shape["ctx"]),
        mesh=mesh,
        in_specs=(split, split, split, P("grp"), P()),
        out_specs=split,
        check_vma=False,
    )
```

```python
import functools

import jax
import jax.numpy as jnp
from jax import lax
from jax.experimental import pallas as pl
from jax.experimental.pallas import tpu as pltpu
from jax.sharding import PartitionSpec as P

HEADS = 12
HDIM = 64
LEVELS = 4
PAIRS = 2 * LEVELS * HDIM
MESH = pl.DeviceIdType.MESH
NT = (((1,), (1,)), ((), ()))
F32 = jnp.float32
BF16 = jnp.bfloat16
FAR_FIRST = (2, 1, 3)


def kernel(
    n, q_hbm, k_hbm, v_hbm, len_hbm, w_hbm, out_ref,
    len_ref, q_in, k_in, v_in, kv2, kv1, q2, q1, kv1_send, q1_send, o2, o1, o2_send, o1_send, w_buf,
    in_sem, own_sem, w_sem,
    one_send, kv2_recv, hop2_recv, hop2_send, kv1_recv, hop1_send, q2_recv, q1_recv, o2_recv, o1_recv,
):
    rows = out_ref.shape[0]
    half = rows // 2
    cols = n // LEVELS
    chips = cols // 2
    me = lax.axis_index("ctx")
    level, col = me // cols, me % cols
    core = col % 2
    flip = 1 - 2 * core
    sibling = me + flip
    low = lax.broadcasted_iota(jnp.int32, (1, 2 * HDIM), 1) < HDIM

    def up(off):
        return (level + off) % LEVELS

    def source(off):
        return (level + LEVELS - off) % LEVELS

    def chip_col(off):
        return (col + 2 * off) % cols

    def pair(ref, g):
        return ref.at[:, pl.ds(pl.multiple_of(g * 2 * HDIM, 2 * HDIM), 2 * HDIM)]

    local = [
        pltpu.make_async_copy(hbm.at[:, pl.ds(PAIRS, LEVELS * HDIM)], ref, in_sem.at[i])
        for i, (hbm, ref) in enumerate(((k_hbm, k_in), (v_hbm, v_in), (q_hbm, q_in)))
    ]
    own = [
        pltpu.make_async_copy(pair(k_hbm, level), kv2.at[me, 0], own_sem.at[0]),
        pltpu.make_async_copy(pair(v_hbm, level), kv2.at[me, 1], own_sem.at[1]),
        pltpu.make_async_copy(pair(q_hbm, level), q2.at[level], own_sem.at[2]),
        pltpu.make_async_copy(len_hbm, len_ref, own_sem.at[3]),
    ]
    w_copy = pltpu.make_async_copy(w_hbm, w_buf, w_sem)
    for copy in local + own:
        copy.start()

    barrier = pltpu.get_barrier_semaphore()
    greeted = [up(off) * cols + col for off in range(1, LEVELS)] + [sibling]
    greeted += [level * cols + chip_col(off) for off in range(1, chips)]
    for other in greeted:
        pl.semaphore_signal(barrier, inc=1, device_id={"ctx": other}, device_id_type=MESH)

    for copy in local:
        copy.wait()
    for g in range(LEVELS):
        one = slice(HDIM * g, HDIM * g + HDIM)
        kv1_send[g] = jnp.concatenate([k_in[:, one], v_in[:, one]], axis=1)
        q_one = q_in[:, one].astype(F32)
        q1_send[g] = jnp.concatenate([q_one[:half], q_one[half:]], axis=1).astype(BF16)
    kv1[me] = kv1_send[level]
    q1[level] = q1_send[level]

    pl.semaphore_wait(barrier, len(greeted))

    sent = []

    def remote(src, dst, send_sem, recv_sem, target):
        copy = pltpu.make_async_remote_copy(
            src_ref=src, dst_ref=dst, send_sem=send_sem, recv_sem=recv_sem,
            device_id={"ctx": target}, device_id_type=MESH,
        )
        copy.start()
        sent.append(copy)

    def arrived(buf, sem):
        pltpu.make_async_remote_copy(
            src_ref=buf, dst_ref=buf, send_sem=sem, recv_sem=sem,
            device_id={"ctx": sibling}, device_id_type=MESH,
        ).wait_recv()

    def send(src, dst, kind, off, recv_sem):
        remote(src, dst, one_send.at[kind, off], recv_sem, up(off) * cols + col)

    def send_pair(off):
        send(pair(k_hbm, up(off)), kv2.at[me, 0], 0, off, kv2_recv.at[level, 0])
        send(pair(v_hbm, up(off)), kv2.at[me, 1], 1, off, kv2_recv.at[level, 1])
        send(pair(q_hbm, up(off)), q2.at[level], 2, off, q2_recv.at[level])

    def send_single(off):
        send(kv1_send.at[up(off)], kv1.at[me], 3, off, kv1_recv.at[me])
        send(q1_send.at[up(off)], q1.at[level], 4, off, q1_recv.at[level])

    used = [0, 0]
    stages = ((kv2, hop2_send, hop2_recv), (kv1, hop1_send, kv1_recv))

    def forward(stage, slot, target):
        buf, send_sem, recv_sem = stages[stage]
        remote(buf.at[slot], buf.at[slot], send_sem.at[used[stage]], recv_sem.at[slot], target)
        used[stage] += 1

    def spread(stage, slot):
        for off in range(1, chips):
            forward(stage, slot, level * cols + chip_col(off))
        forward(stage, slot, sibling)

    def from_column(stage, off):
        slot = source(off) * cols + col
        if stage == 0:
            arrived(kv2.at[slot, 0], kv2_recv.at[source(off), 0])
            arrived(kv2.at[slot, 1], kv2_recv.at[source(off), 1])
        else:
            arrived(kv1.at[slot], kv1_recv.at[slot])
        spread(stage, slot)

    def from_chips(stage):
        buf, _, recv_sem = stages[stage]
        for off in (0,) + FAR_FIRST:
            for hop in range(1, chips):
                slot = source(off) * cols + chip_col(hop)
                arrived(buf.at[slot], recv_sem.at[slot])
                forward(stage, slot, sibling)

    def from_sibling(stage):
        buf, _, recv_sem = stages[stage]
        for off in (0,) + FAR_FIRST:
            for hop in range(chips):
                slot = source(off) * cols + chip_col(hop) + flip
                arrived(buf.at[slot], recv_sem.at[slot])

    for off in FAR_FIRST:
        send_pair(off)
    for copy in own:
        copy.wait()
    w_copy.start()
    spread(0, me)
    spread(1, me)
    for off in FAR_FIRST:
        send_single(off)
    for off in FAR_FIRST:
        from_column(0, off)
    for off in FAR_FIRST:
        from_column(1, off)
    from_chips(0)
    from_sibling(0)

    valid = len_ref[0]
    frames = n * rows
    scale = jnp.asarray(HDIM ** -0.5, BF16)
    live = lax.broadcasted_iota(jnp.int32, (1, frames), 1) < valid

    def attend(q, k, v):
        s = lax.dot_general(q, k, NT, preferred_element_type=F32)
        s = jnp.where(live, s, F32(-1e30))
        e = jnp.exp(s - jnp.max(s, axis=1, keepdims=True))
        total = jnp.sum(e, axis=1, keepdims=True)
        return jnp.dot(e.astype(BF16), v, preferred_element_type=F32) / total

    def keep(j, out):
        row = (j * cols + col) * rows + lax.broadcasted_iota(jnp.int32, (rows, 1), 0)
        return jnp.where(row < valid, out, F32(0.0))

    def attend_pair(off):
        j = up(off)
        if off:
            arrived(q2.at[j], q2_recv.at[j])
        q = q2[j] * scale
        zero = jnp.zeros_like(q)
        q = jnp.concatenate([jnp.where(low, q, zero), jnp.where(low, zero, q)], axis=0)
        out = attend(q, kv2[:, 0].reshape(frames, 2 * HDIM), kv2[:, 1].reshape(frames, 2 * HDIM))
        out = keep(j, jnp.where(low, out[:rows], out[rows:])).astype(BF16)
        if off:
            o2_send[off] = out
            send(o2_send.at[off], o2.at[level], 5, off, o2_recv.at[level])
        else:
            o2[level] = out

    def attend_single(off):
        j = up(off)
        if off:
            arrived(q1.at[j], q1_recv.at[j])
        q = q1[j].astype(F32)
        zero = jnp.zeros_like(q)
        q = jnp.concatenate(
            [jnp.where(low, q, zero), jnp.where(low, pltpu.roll(q, HDIM, 1), zero)], axis=0
        ).astype(BF16) * scale
        kv = kv1[...].reshape(frames, 2 * HDIM)
        out = keep(j, attend(q, kv, kv))
        out = jnp.where(low, pltpu.roll(out[half:], HDIM, 1), out[:half]).astype(BF16)
        if off:
            o1_send[off] = out
            send(o1_send.at[off], o1.at[level], 6, off, o1_recv.at[level])
        else:
            o1[level] = out

    attend_pair(FAR_FIRST[0])
    attend_pair(FAR_FIRST[1])
    from_chips(1)
    attend_pair(FAR_FIRST[2])
    attend_pair(0)
    from_sibling(1)
    for off in FAR_FIRST + (0,):
        attend_single(off)

    w_copy.wait()
    for off in FAR_FIRST:
        arrived(o2.at[source(off)], o2_recv.at[source(off)])
    pairs = jnp.concatenate([o2[g] for g in range(LEVELS)], axis=1)
    total = jnp.dot(pairs, w_buf[:PAIRS, :], preferred_element_type=F32)
    for off in FAR_FIRST:
        arrived(o1.at[source(off)], o1_recv.at[source(off)])
    parts = []
    for g in range(0, LEVELS, 2):
        even, odd = o1[g].astype(F32), o1[g + 1].astype(F32)
        top = jnp.where(low, pltpu.roll(even, HDIM, 1), odd)
        bottom = jnp.where(low, even, pltpu.roll(odd, HDIM, 1))
        parts.append(jnp.concatenate([top, bottom], axis=0).astype(BF16))
    singles = jnp.concatenate(parts, axis=1)
    total = total + jnp.dot(singles, w_buf[PAIRS:, :], preferred_element_type=F32)
    out_ref[...] = total.astype(BF16)
    for copy in sent:
        copy.wait_send()


def body(n, query_in, key_in, value_in, length, out_weight):
    rows, cin = query_in.shape
    width = out_weight.shape[1]
    chips = n // LEVELS // 2
    hops = LEVELS * chips + LEVELS * (chips - 1)
    lanes = 2 * HDIM
    dma = pltpu.SemaphoreType.DMA
    hbm = pl.BlockSpec(memory_space=pl.ANY)

    def vmem(*shape):
        return pltpu.VMEM(shape, BF16)

    return pl.pallas_call(
        functools.partial(kernel, n),
        out_shape=pltpu.VMEM((rows, width), BF16),
        in_specs=[hbm] * 5,
        out_specs=pl.BlockSpec(memory_space=pltpu.VMEM),
        scratch_shapes=[
            pltpu.SMEM((1,), jnp.int32),
            vmem(rows, LEVELS * HDIM),
            vmem(rows, LEVELS * HDIM),
            vmem(rows, LEVELS * HDIM),
            vmem(n, 2, rows, lanes),
            vmem(n, rows, lanes),
            vmem(LEVELS, rows, lanes),
            vmem(LEVELS, rows // 2, lanes),
            vmem(LEVELS, rows, lanes),
            vmem(LEVELS, rows // 2, lanes),
            vmem(LEVELS, rows, lanes),
            vmem(LEVELS, rows // 2, lanes),
            vmem(LEVELS, rows, lanes),
            vmem(LEVELS, rows // 2, lanes),
            vmem(cin, width),
            dma((3,)),
            dma((4,)),
            dma,
            dma((7, LEVELS)),
            dma((LEVELS, 2)),
            dma((n,)),
            dma((hops,)),
            dma((n,)),
            dma((hops,)),
            dma((LEVELS,)),
            dma((LEVELS,)),
            dma((LEVELS,)),
            dma((LEVELS,)),
        ],
        compiler_params=pltpu.CompilerParams(
            collective_id=0, has_side_effects=True, vmem_limit_bytes=63 * 2**20
        ),
        name="attention",
    )(query_in, key_in, value_in, length, out_weight)


def solution(mesh):
    split = P(("grp", "ctx"), None)
    return jax.shard_map(
        functools.partial(body, mesh.shape["ctx"]),
        mesh=mesh,
        in_specs=(split, split, split, P("grp"), P()),
        out_specs=split,
        check_vma=False,
    )
```

```python
import functools

import jax
import jax.numpy as jnp
from jax import lax
from jax.experimental import pallas as pl
from jax.experimental.pallas import tpu as pltpu
from jax.sharding import PartitionSpec as P

HEADS = 12
HDIM = 64
LEVELS = 4
PAIRS = 2 * LEVELS * HDIM
MESH = pl.DeviceIdType.MESH
NT = (((1,), (1,)), ((), ()))
F32 = jnp.float32
BF16 = jnp.bfloat16
FAR_FIRST = (2, 1, 3)


def kernel(
    n, q_hbm, k_hbm, v_hbm, len_hbm, w_hbm, out_ref,
    len_ref, q_in, k_in, v_in, kv2, kv1, q2, q1, kv1_send, q1_send, o2, o1, o2_send, o1_send, w_buf,
    in_sem, own_sem, w_sem,
    one_send, kv2_recv, hop2_recv, hop2_send, kv1_recv, hop1_send, q2_recv, q1_recv, o2_recv, o1_recv,
):
    rows = out_ref.shape[0]
    half = rows // 2
    cols = n // LEVELS
    chips = cols // 2
    me = lax.axis_index("ctx")
    level, col = me // cols, me % cols
    core = col % 2
    flip = 1 - 2 * core
    sibling = me + flip
    low = lax.broadcasted_iota(jnp.int32, (1, 2 * HDIM), 1) < HDIM

    def up(off):
        return (level + off) % LEVELS

    def source(off):
        return (level + LEVELS - off) % LEVELS

    def chip_col(off):
        return (col + 2 * off) % cols

    def pair(ref, g):
        return ref.at[:, pl.ds(pl.multiple_of(g * 2 * HDIM, 2 * HDIM), 2 * HDIM)]

    local = [
        pltpu.make_async_copy(hbm.at[:, pl.ds(PAIRS, LEVELS * HDIM)], ref, in_sem.at[i])
        for i, (hbm, ref) in enumerate(((k_hbm, k_in), (v_hbm, v_in), (q_hbm, q_in)))
    ]
    own = [
        pltpu.make_async_copy(pair(k_hbm, level), kv2.at[me, 0], own_sem.at[0]),
        pltpu.make_async_copy(pair(v_hbm, level), kv2.at[me, 1], own_sem.at[1]),
        pltpu.make_async_copy(pair(q_hbm, level), q2.at[level], own_sem.at[2]),
        pltpu.make_async_copy(len_hbm, len_ref, own_sem.at[3]),
    ]
    w_copy = pltpu.make_async_copy(w_hbm, w_buf, w_sem)
    for copy in local + own:
        copy.start()

    barrier = pltpu.get_barrier_semaphore()
    greeted = [up(off) * cols + col for off in range(1, LEVELS)] + [sibling]
    greeted += [level * cols + chip_col(off) for off in range(1, chips)]
    for other in greeted:
        pl.semaphore_signal(barrier, inc=1, device_id={"ctx": other}, device_id_type=MESH)

    for copy in local:
        copy.wait()
    for g in range(LEVELS):
        one = slice(HDIM * g, HDIM * g + HDIM)
        kv1_send[g] = jnp.concatenate([k_in[:, one], v_in[:, one]], axis=1)
        q_one = q_in[:, one].astype(F32)
        q1_send[g] = jnp.concatenate([q_one[:half], q_one[half:]], axis=1).astype(BF16)
    kv1[me] = kv1_send[level]
    q1[level] = q1_send[level]

    pl.semaphore_wait(barrier, len(greeted))

    sent = []

    def remote(src, dst, send_sem, recv_sem, target):
        copy = pltpu.make_async_remote_copy(
            src_ref=src, dst_ref=dst, send_sem=send_sem, recv_sem=recv_sem,
            device_id={"ctx": target}, device_id_type=MESH,
        )
        copy.start()
        sent.append(copy)

    def arrived(buf, sem):
        pltpu.make_async_remote_copy(
            src_ref=buf, dst_ref=buf, send_sem=sem, recv_sem=sem,
            device_id={"ctx": sibling}, device_id_type=MESH,
        ).wait_recv()

    def send(src, dst, kind, off, recv_sem):
        remote(src, dst, one_send.at[kind, off], recv_sem, up(off) * cols + col)

    def send_pair(off):
        send(pair(k_hbm, up(off)), kv2.at[me, 0], 0, off, kv2_recv.at[level, 0])
        send(pair(v_hbm, up(off)), kv2.at[me, 1], 1, off, kv2_recv.at[level, 1])
        send(pair(q_hbm, up(off)), q2.at[level], 2, off, q2_recv.at[level])

    def send_single(off):
        send(kv1_send.at[up(off)], kv1.at[me], 3, off, kv1_recv.at[me])
        send(q1_send.at[up(off)], q1.at[level], 4, off, q1_recv.at[level])

    used = [0, 0]
    stages = ((kv2, hop2_send, hop2_recv), (kv1, hop1_send, kv1_recv))

    def forward(stage, slot, target):
        buf, send_sem, recv_sem = stages[stage]
        remote(buf.at[slot], buf.at[slot], send_sem.at[used[stage]], recv_sem.at[slot], target)
        used[stage] += 1

    def spread(stage, slot):
        for off in range(1, chips):
            forward(stage, slot, level * cols + chip_col(off))
        forward(stage, slot, sibling)

    def from_column(stage, off):
        slot = source(off) * cols + col
        if stage == 0:
            arrived(kv2.at[slot, 0], kv2_recv.at[source(off), 0])
            arrived(kv2.at[slot, 1], kv2_recv.at[source(off), 1])
        else:
            arrived(kv1.at[slot], kv1_recv.at[slot])
        spread(stage, slot)

    def from_chips(stage):
        buf, _, recv_sem = stages[stage]
        for off in (0,) + FAR_FIRST:
            for hop in range(1, chips):
                slot = source(off) * cols + chip_col(hop)
                arrived(buf.at[slot], recv_sem.at[slot])
                forward(stage, slot, sibling)

    def from_sibling(stage):
        buf, _, recv_sem = stages[stage]
        for off in (0,) + FAR_FIRST:
            for hop in range(chips):
                slot = source(off) * cols + chip_col(hop) + flip
                arrived(buf.at[slot], recv_sem.at[slot])

    for off in FAR_FIRST:
        send_pair(off)
    for copy in own:
        copy.wait()
    spread(0, me)
    spread(1, me)
    for off in FAR_FIRST:
        send_single(off)
    for off in FAR_FIRST:
        from_column(0, off)
    for off in FAR_FIRST:
        from_column(1, off)
    w_copy.start()
    from_chips(0)
    from_sibling(0)

    valid = len_ref[0]
    frames = n * rows
    scale = jnp.asarray(HDIM ** -0.5, BF16)
    live = lax.broadcasted_iota(jnp.int32, (1, frames), 1) < valid

    def attend(q, k, v):
        s = lax.dot_general(q, k, NT, preferred_element_type=F32)
        s = jnp.where(live, s, F32(-1e30))
        e = jnp.exp(s - jnp.max(s, axis=1, keepdims=True))
        total = jnp.sum(e, axis=1, keepdims=True)
        return jnp.dot(e.astype(BF16), v, preferred_element_type=F32) / total

    def keep(j, out):
        row = (j * cols + col) * rows + lax.broadcasted_iota(jnp.int32, (rows, 1), 0)
        return jnp.where(row < valid, out, F32(0.0))

    def attend_pair(off):
        j = up(off)
        if off:
            arrived(q2.at[j], q2_recv.at[j])
        q = q2[j] * scale
        zero = jnp.zeros_like(q)
        q = jnp.concatenate([jnp.where(low, q, zero), jnp.where(low, zero, q)], axis=0)
        out = attend(q, kv2[:, 0].reshape(frames, 2 * HDIM), kv2[:, 1].reshape(frames, 2 * HDIM))
        out = keep(j, jnp.where(low, out[:rows], out[rows:])).astype(BF16)
        if off:
            o2_send[off] = out
            send(o2_send.at[off], o2.at[level], 5, off, o2_recv.at[level])
        else:
            o2[level] = out

    def attend_single(off):
        j = up(off)
        if off:
            arrived(q1.at[j], q1_recv.at[j])
        q = q1[j].astype(F32)
        zero = jnp.zeros_like(q)
        q = jnp.concatenate(
            [jnp.where(low, q, zero), jnp.where(low, pltpu.roll(q, HDIM, 1), zero)], axis=0
        ).astype(BF16) * scale
        kv = kv1[...].reshape(frames, 2 * HDIM)
        out = keep(j, attend(q, kv, kv))
        out = jnp.where(low, pltpu.roll(out[half:], HDIM, 1), out[:half]).astype(BF16)
        if off:
            o1_send[off] = out
            send(o1_send.at[off], o1.at[level], 6, off, o1_recv.at[level])
        else:
            o1[level] = out

    attend_pair(FAR_FIRST[0])
    attend_pair(FAR_FIRST[1])
    from_chips(1)
    attend_pair(FAR_FIRST[2])
    attend_pair(0)
    from_sibling(1)
    for off in FAR_FIRST + (0,):
        attend_single(off)

    w_copy.wait()
    for off in FAR_FIRST:
        arrived(o2.at[source(off)], o2_recv.at[source(off)])
    pairs = jnp.concatenate([o2[g] for g in range(LEVELS)], axis=1)
    total = jnp.dot(pairs, w_buf[:PAIRS, :], preferred_element_type=F32)
    for off in FAR_FIRST:
        arrived(o1.at[source(off)], o1_recv.at[source(off)])
    parts = []
    for g in range(0, LEVELS, 2):
        even, odd = o1[g].astype(F32), o1[g + 1].astype(F32)
        top = jnp.where(low, pltpu.roll(even, HDIM, 1), odd)
        bottom = jnp.where(low, even, pltpu.roll(odd, HDIM, 1))
        parts.append(jnp.concatenate([top, bottom], axis=0).astype(BF16))
    singles = jnp.concatenate(parts, axis=1)
    total = total + jnp.dot(singles, w_buf[PAIRS:, :], preferred_element_type=F32)
    out_ref[...] = total.astype(BF16)
    for copy in sent:
        copy.wait_send()


def body(n, query_in, key_in, value_in, length, out_weight):
    rows, cin = query_in.shape
    width = out_weight.shape[1]
    chips = n // LEVELS // 2
    hops = LEVELS * chips + LEVELS * (chips - 1)
    lanes = 2 * HDIM
    dma = pltpu.SemaphoreType.DMA
    hbm = pl.BlockSpec(memory_space=pl.ANY)

    def vmem(*shape):
        return pltpu.VMEM(shape, BF16)

    return pl.pallas_call(
        functools.partial(kernel, n),
        out_shape=pltpu.VMEM((rows, width), BF16),
        in_specs=[hbm] * 5,
        out_specs=pl.BlockSpec(memory_space=pltpu.VMEM),
        scratch_shapes=[
            pltpu.SMEM((1,), jnp.int32),
            vmem(rows, LEVELS * HDIM),
            vmem(rows, LEVELS * HDIM),
            vmem(rows, LEVELS * HDIM),
            vmem(n, 2, rows, lanes),
            vmem(n, rows, lanes),
            vmem(LEVELS, rows, lanes),
            vmem(LEVELS, rows // 2, lanes),
            vmem(LEVELS, rows, lanes),
            vmem(LEVELS, rows // 2, lanes),
            vmem(LEVELS, rows, lanes),
            vmem(LEVELS, rows // 2, lanes),
            vmem(LEVELS, rows, lanes),
            vmem(LEVELS, rows // 2, lanes),
            vmem(cin, width),
            dma((3,)),
            dma((4,)),
            dma,
            dma((7, LEVELS)),
            dma((LEVELS, 2)),
            dma((n,)),
            dma((hops,)),
            dma((n,)),
            dma((hops,)),
            dma((LEVELS,)),
            dma((LEVELS,)),
            dma((LEVELS,)),
            dma((LEVELS,)),
        ],
        compiler_params=pltpu.CompilerParams(
            collective_id=0, has_side_effects=True, vmem_limit_bytes=63 * 2**20
        ),
        name="attention",
    )(query_in, key_in, value_in, length, out_weight)


def solution(mesh):
    split = P(("grp", "ctx"), None)
    return jax.shard_map(
        functools.partial(body, mesh.shape["ctx"]),
        mesh=mesh,
        in_specs=(split, split, split, P("grp"), P()),
        out_specs=split,
        check_vma=False,
    )
```
